32 devices in a mesh: dp: 8 (over z, x), tensor: 4 (over y, core).
Axes of the slice: x: 2, y: 2, z: 4, core: 2. Of those that a mesh axis runs over, the one named last changes fastest.
Arguments:
- tokens: bfloat16 [16384, 768], P(('dp', 'tensor')), may hold values from -6 to 6
- context: bfloat16 [4096, 768], P(('dp', 'tensor')), may hold values from -6 to 6
- segment_ids: int32 [16384], P('dp'), may hold values from 0 to 3, as said below
- frame_ids: int32 [16384], P('dp'), may hold values from 0 to 63, as said below
- context_lengths: int32 [32], P('dp'), may hold values from 1 to 256, as said below
- cross_gain: float32 [768], replicated, may hold values from 0.25 to 1.75
- cross_bias: float32 [768], replicated, may hold values from -1.75 to 1.75
- cross_query: bfloat16 [768, 768], P(None, 'tensor'), may hold values from -0.21875 to 0.21875
- cross_key: bfloat16 [768, 768], P(None, 'tensor'), may hold values from -0.21875 to 0.21875
- cross_value: bfloat16 [768, 768], P(None, 'tensor'), may hold values from -0.21875 to 0.21875
- cross_out: bfloat16 [768, 768], P('tensor'), may hold values from -1.75 to 1.75
- attn_gain: float32 [768], replicated, may hold values from 0.25 to 1.75
- attn_bias: float32 [768], replicated, may hold values from -1.75 to 1.75
- attn_query: bfloat16 [768, 768], P(None, 'tensor'), may hold values from -0.21875 to 0.21875
- attn_key: bfloat16 [768, 768], P(None, 'tensor'), may hold values from -0.21875 to 0.21875
- attn_value: bfloat16 [768, 768], P(None, 'tensor'), may hold values from -0.21875 to 0.21875
- attn_out: bfloat16 [768, 768], P('tensor'), may hold values from -1.75 to 1.75
- mlp_gain: float32 [768], replicated, may hold values from 0.25 to 1.75
- mlp_bias: float32 [768], replicated, may hold values from -1.75 to 1.75
- mlp_up: bfloat16 [768, 3072], P(None, 'tensor'), may hold values from -0.21875 to 0.21875
- mlp_down: bfloat16 [3072, 768], P('tensor'), may hold values from -0.109375 to 0.109375
- out_grad: bfloat16 [16384, 768], P(('dp', 'tensor')), may hold values from -6 to 6
Outputs:
- block_out: bfloat16 [16384, 768], P(('dp', 'tensor'))
- tokens_grad: float32 [16384, 768], P(('dp', 'tensor'))
- context_grad: float32 [4096, 768], P(('dp', 'tensor'))
- cross_gain_grad: float32 [768], replicated
- cross_bias_grad: float32 [768], replicated
- cross_query_grad: float32 [768, 768], P(None, 'tensor')
- cross_key_grad: float32 [768, 768], P(None, 'tensor')
- cross_value_grad: float32 [768, 768], P(None, 'tensor')
- cross_out_grad: float32 [768, 768], P('tensor')
- attn_gain_grad: float32 [768], replicated
- attn_bias_grad: float32 [768], replicated
- attn_query_grad: float32 [768, 768], P(None, 'tensor')
- attn_key_grad: float32 [768, 768], P(None, 'tensor')
- attn_value_grad: float32 [768, 768], P(None, 'tensor')
- attn_out_grad: float32 [768, 768], P('tensor')
- mlp_gain_grad: float32 [768], replicated
- mlp_bias_grad: float32 [768], replicated
- mlp_up_grad: float32 [768, 3072], P(None, 'tensor')
- mlp_down_grad: float32 [3072, 768], P('tensor')
The draws below stay inside these ranges and needn't reach their ends.
Inputs may be any that keep to these rules, and one draw needn't show every extreme that they name: `segment_ids`: within each aligned block of 2048 positions (one group) the ids never fall and take every value 0 to 3; every clip's token count is a multiple of its group's frame size, and each group has a clip of exactly 1024 tokens. `frame_ids`: groups alternate between frames of 64 tokens and frames of 16 tokens (which comes first is drawn); a token's frame id is its position within its clip divided by its group's frame size, rounded down. `context_lengths`: the 4 lengths of each group sum to 512, and each group has one of exactly 256; clip c's context features follow those of clips 0 to c - 1 in its group's block of context.
All inputs are finite; a program needn't handle non-finite values.
Results may differ from the reference program's by a relative error of at most 0.03.
Values may be sent and summed in bfloat16 or wider, within the bound.
No kernel may reach another device: no remote copies, remote signals or barrier semaphores. Data moves between devices by JAX's collectives and lax.ppermute only.
A program may use at most 128 MiB of HBM per device.

```python
import jax
import jax.numpy as jnp
from jax import lax

D = 768
HEAD_DIM = 64
FF = 3072
TOK_DEV = 2048
SEQ_MOST = 1024
FRAME_LO = 16
FRAME_HI = 64
CTX_MOST = 256
CLIPS = 4
CTX_DEV = 512
TOKENS = 16384
CTX_ALL = 4096
CLIPS_ALL = 32


def split_lengths(rng_key, longest, pieces):
    first_key, second_key, third_key, fourth_key = jax.random.split(rng_key, 4)
    first_cut = jax.random.randint(first_key, (), 1, longest - 1)
    second_cut = jax.random.randint(second_key, (), 1, longest - first_cut)
    third_cut = longest - first_cut - second_cut
    pair_count = pieces // 2 - 2
    paired = jax.random.randint(third_key, (pair_count,), 1, longest)
    leading = jnp.stack([jnp.asarray(longest), first_cut, second_cut, third_cut]).astype(jnp.int32)
    joined = jnp.concatenate([leading, paired.astype(jnp.int32), (longest - paired).astype(jnp.int32)])
    shuffle = jax.random.permutation(fourth_key, pieces)
    return joined[shuffle]


def clip_layout(rng_key, group_index):
    parity = jax.random.randint(jax.random.fold_in(rng_key, 7), (), 0, 2)
    high_res = (group_index + parity) % 2
    frame_size = jnp.where(high_res == 1, FRAME_HI, FRAME_LO).astype(jnp.int32)
    frames = split_lengths(jax.random.fold_in(jax.random.fold_in(rng_key, 11), group_index), SEQ_MOST // frame_size, CLIPS)
    lengths = frames * frame_size
    clip_ends = jnp.cumsum(lengths).astype(jnp.int32)
    clip_starts = clip_ends - lengths
    position = jnp.arange(TOK_DEV, dtype=jnp.int32)
    segment = jnp.sum((position[:, None] >= clip_ends[None, :]).astype(jnp.int32), axis=1)
    chosen = segment[:, None] == jnp.arange(CLIPS, dtype=jnp.int32)[None, :]
    own_start = jnp.sum(jnp.where(chosen, clip_starts[None, :], 0), axis=1)
    frame_id = (position - own_start) // frame_size
    return (segment.astype(jnp.int32), frame_id.astype(jnp.int32))


def draw_segment_ids(key, part):
    group_ids = jnp.arange(TOKENS // TOK_DEV, dtype=jnp.int32)
    segment, frame_id = jax.vmap(lambda group_index: clip_layout(key, group_index))(group_ids)
    return segment.reshape(-1)


def draw_frame_ids(key, part):
    group_ids = jnp.arange(TOKENS // TOK_DEV, dtype=jnp.int32)
    segment, frame_id = jax.vmap(lambda group_index: clip_layout(key, group_index))(group_ids)
    return frame_id.reshape(-1)


def draw_context_lengths(key, part):
    group_ids = jnp.arange(CLIPS_ALL // CLIPS, dtype=jnp.int32)
    lengths = jax.vmap(lambda group_index: split_lengths(jax.random.fold_in(jax.random.fold_in(key, 23), group_index), CTX_MOST, CLIPS))(group_ids)
    return lengths.reshape(-1)


def level_of(rng, shape, shards, least, high):
    factor_of, own = 1.0, jax.random.fold_in(rng, 6)
    for dim, shards_of in shards:
        draws = jnp.exp(jax.random.uniform(jax.random.fold_in(own, dim), (shards_of,), jnp.float32, least / len(shards), high / len(shards)))
        factor_of = factor_of * jnp.repeat(draws, shape[dim] // shards_of).reshape([-1 if axis == dim else 1 for axis in range(len(shape))])
    return factor_of


def bell_draw(stream_key, dims, scale, bound, cuts=(), kind=jnp.bfloat16):
    entries = scale * jax.random.normal(stream_key, dims, jnp.float32)
    if cuts:
        entries = entries * level_of(stream_key, dims, cuts, -0.22, 0.18)
    return jnp.clip(entries, -bound, bound).astype(kind)


def setup_inputs(seed: int = 0) -> dict:
    key_list = jax.random.split(jax.random.key(seed), 23)
    tokens = bell_draw(key_list[0], (TOKENS, D), 1.0, 6.0, ((0, 32),))
    context = bell_draw(key_list[1], (CTX_ALL, D), 1.0, 6.0, ((0, 32),))
    segment_ids = draw_segment_ids(jax.random.fold_in(key_list[22], 71), 0)
    frame_ids = draw_frame_ids(jax.random.fold_in(key_list[22], 71), 0)
    context_lengths = draw_context_lengths(jax.random.fold_in(key_list[22], 71), 0)
    cross_gain = jnp.clip(1.0 + 0.15 * jax.random.normal(key_list[5], (D,), jnp.float32), 0.25, 1.75)
    cross_bias = bell_draw(key_list[6], (D,), 0.3, 1.75, (), jnp.float32)
    cross_query = bell_draw(key_list[7], (D, D), D ** -0.5, 0.21875, ((1, 4),))
    cross_key = bell_draw(key_list[8], (D, D), D ** -0.5, 0.21875, ((1, 4),))
    cross_value = bell_draw(key_list[9], (D, D), D ** -0.5, 0.21875, ((1, 4),))
    cross_out = bell_draw(key_list[10], (D, D), (D // 64) ** -0.5, 1.75, ((0, 4),))
    attn_gain = jnp.clip(1.0 + 0.15 * jax.random.normal(key_list[11], (D,), jnp.float32), 0.25, 1.75)
    attn_bias = bell_draw(key_list[12], (D,), 0.3, 1.75, (), jnp.float32)
    attn_query = bell_draw(key_list[13], (D, D), D ** -0.5, 0.21875, ((1, 4),))
    attn_key = bell_draw(key_list[14], (D, D), D ** -0.5, 0.21875, ((1, 4),))
    attn_value = bell_draw(key_list[15], (D, D), D ** -0.5, 0.21875, ((1, 4),))
    attn_out = bell_draw(key_list[16], (D, D), (D // 64) ** -0.5, 1.75, ((0, 4),))
    mlp_gain = jnp.clip(1.0 + 0.15 * jax.random.normal(key_list[17], (D,), jnp.float32), 0.25, 1.75)
    mlp_bias = bell_draw(key_list[18], (D,), 0.3, 1.75, (), jnp.float32)
    mlp_up = bell_draw(key_list[19], (D, FF), D ** -0.5, 0.21875, ((1, 4),))
    mlp_down = bell_draw(key_list[20], (FF, D), FF ** -0.5, 0.109375, ((0, 4),))
    out_grad = bell_draw(key_list[21], (TOKENS, D), 1.0, 6.0, ((0, 32),))
    return {"tokens": tokens, "context": context, "segment_ids": segment_ids, "frame_ids": frame_ids, "context_lengths": context_lengths, "cross_gain": cross_gain, "cross_bias": cross_bias, "cross_query": cross_query, "cross_key": cross_key, "cross_value": cross_value, "cross_out": cross_out, "attn_gain": attn_gain, "attn_bias": attn_bias, "attn_query": attn_query, "attn_key": attn_key, "attn_value": attn_value, "attn_out": attn_out, "mlp_gain": mlp_gain, "mlp_bias": mlp_bias, "mlp_up": mlp_up, "mlp_down": mlp_down, "out_grad": out_grad}


@jax.custom_vjp
def low(v):
    return lax.optimization_barrier(v.astype(jnp.bfloat16)).astype(jnp.float32)

@jax.custom_vjp
def low_back(v):
    return v

def low_keep(v):
    return (low(v), None)

def low_pass(kept, grad):
    return (grad,)

def back_keep(v):
    return (v, None)

def back_low(kept, grad):
    return (low(grad),)
low.defvjp(low_keep, low_pass)
low_back.defvjp(back_keep, back_low)
EPSILON = 1e-05
PRECISE = lax.Precision.HIGHEST

def matmul(left, right):
    return jnp.dot(left, right, precision=PRECISE)

def layer_norm(inputs, norm_gain, norm_bias):
    average = lax.optimization_barrier(jnp.mean(inputs, axis=-1, keepdims=True))
    centred = inputs - average
    variance = lax.optimization_barrier(jnp.mean(centred * centred, axis=-1, keepdims=True))
    return centred * lax.rsqrt(variance + EPSILON) * norm_gain + norm_bias

def attention(queries, key_rows, value_rows, allowed):
    query_count = queries.shape[0]
    block_rows = min(512, query_count)
    block_count = query_count // block_rows
    head_count = queries.shape[1] // HEAD_DIM
    score_scale = HEAD_DIM ** (-0.5)
    key_heads = key_rows.reshape(key_rows.shape[0], head_count, HEAD_DIM)
    value_heads = value_rows.reshape(value_rows.shape[0], head_count, HEAD_DIM)

    def one_block(paired):
        query_block, allowed_block = paired
        query_heads = query_block.reshape(block_rows, head_count, HEAD_DIM)
        scores = jnp.einsum('qhd,khd->hqk', query_heads, key_heads, precision=PRECISE) * score_scale
        scores = low_back(scores)
        scores = jnp.where(allowed_block[None], scores, -1e+30)
        row_max = lax.optimization_barrier(jnp.max(scores, axis=-1, keepdims=True))
        exp_scores = jnp.exp(scores - row_max)
        weights_low = low(exp_scores / lax.optimization_barrier(jnp.sum(exp_scores, axis=-1, keepdims=True)))
        outputs = jnp.einsum('hqk,khd->qhd', weights_low, value_heads, precision=PRECISE)
        return outputs.reshape(block_rows, head_count * HEAD_DIM)
    mixed_blocks = lax.map(jax.checkpoint(one_block), (queries.reshape(block_count, block_rows, -1), allowed.reshape(block_count, block_rows, -1)))
    return mixed_blocks.reshape(query_count, -1)

def group_forward(params, group_tokens, group_context, segment, frame_id, lengths):
    cross_gain, cross_bias, cross_query, cross_key, cross_value, cross_out, attn_gain, attn_bias, attn_query, attn_key, attn_value, attn_out, mlp_gain, mlp_bias, mlp_up, mlp_down = params
    clip_ends = jnp.cumsum(lengths).astype(jnp.int32)
    context_ids = jnp.arange(group_context.shape[0]).astype(jnp.int32)
    context_clip = lax.optimization_barrier(jnp.sum((context_ids[:, None] >= clip_ends[None, :]).astype(jnp.int32), axis=1)).astype(jnp.int32)
    cross_allowed = segment[:, None] == context_clip[None, :]
    self_allowed = (segment[:, None] == segment[None, :]) & (frame_id[None, :] <= frame_id[:, None])
    normed1 = low(layer_norm(group_tokens, cross_gain, cross_bias))
    query1 = low(low_back(matmul(normed1, cross_query)))
    key1 = low(low_back(matmul(group_context, cross_key)))
    value1 = low(low_back(matmul(group_context, cross_value)))
    mixed1 = low(low_back(attention(query1, key1, value1, cross_allowed)))
    hidden1 = group_tokens + low_back(matmul(mixed1, cross_out))
    normed2 = low(layer_norm(hidden1, attn_gain, attn_bias))
    query2 = low(low_back(matmul(normed2, attn_query)))
    key2 = low(low_back(matmul(normed2, attn_key)))
    value2 = low(low_back(matmul(normed2, attn_value)))
    mixed2 = low(low_back(attention(query2, key2, value2, self_allowed)))
    hidden2 = hidden1 + low_back(matmul(mixed2, attn_out))
    normed3 = low(layer_norm(hidden2, mlp_gain, mlp_bias))
    upper_rows = low_back(matmul(normed3, mlp_up))
    activated = low(jax.nn.gelu(upper_rows, approximate=True))
    return hidden2 + low_back(matmul(activated, mlp_down))

def reference(tokens, context, segment_ids, frame_ids, context_lengths, cross_gain, cross_bias, cross_query, cross_key, cross_value, cross_out, attn_gain, attn_bias, attn_query, attn_key, attn_value, attn_out, mlp_gain, mlp_bias, mlp_up, mlp_down, out_grad):
    group_count = segment_ids.shape[0] // TOK_DEV
    params = tuple((weight.astype(jnp.float32) for weight in (cross_gain, cross_bias, cross_query, cross_key, cross_value, cross_out, attn_gain, attn_bias, attn_query, attn_key, attn_value, attn_out, mlp_gain, mlp_bias, mlp_up, mlp_down)))
    token_groups = tokens.astype(jnp.float32).reshape(group_count, TOK_DEV, D)
    context_groups = context.astype(jnp.float32).reshape(group_count, CTX_DEV, D)
    segment_groups = segment_ids.reshape(group_count, TOK_DEV)
    frame_groups = frame_ids.reshape(group_count, TOK_DEV)
    length_groups = context_lengths.reshape(group_count, CLIPS)

    def forward(weights, token_values, context_values):

        def one_group(bundle):
            group_tokens, group_context, segment, frame_id, lengths = bundle
            return group_forward(weights, group_tokens, group_context, segment, frame_id, lengths)
        return lax.map(jax.checkpoint(one_group), (token_values, context_values, segment_groups, frame_groups, length_groups))
    outputs, pullback = jax.vjp(forward, params, token_groups, context_groups)
    weight_grads, token_grads, context_grads = pullback(out_grad.astype(jnp.float32).reshape(group_count, TOK_DEV, D))
    return (outputs.reshape(-1, D).astype(jnp.bfloat16), token_grads.reshape(-1, D), context_grads.reshape(-1, D), weight_grads[0], weight_grads[1], weight_grads[2], weight_grads[3], weight_grads[4], weight_grads[5], weight_grads[6], weight_grads[7], weight_grads[8], weight_grads[9], weight_grads[10], weight_grads[11], weight_grads[12], weight_grads[13], weight_grads[14], weight_grads[15])
```

```python
import functools

import jax
import jax.numpy as jnp
from jax import lax
from jax.experimental import pallas as pl
from jax.experimental.pallas import tpu as pltpu
from jax.sharding import PartitionSpec as P

HEAD_DIM = 64
EPSILON = 1e-05
BLOCK = 256
WIDE = 256
FAR = -(2.0**100)
LOW = jnp.bfloat16
F32 = jnp.float32


def dot(left, right, left_dim, right_dim):
    return lax.dot_general(
        left, right, (((left_dim,), (right_dim,)), ((), ())), preferred_element_type=F32
    )


def swap(values, axis, bit):
    size = lax.axis_size(axis)
    return lax.ppermute(values, axis, [(i, i ^ bit) for i in range(size)])


def gather_pieces(own):
    near = swap(own, "tensor", 1)
    far = swap(own, "tensor", 2)
    return [own, near, far, swap(far, "tensor", 1)]


def reduce_pieces(pieces):
    pieces = lax.optimization_barrier(tuple(piece.astype(LOW) for piece in pieces))
    near_own = swap(pieces[1], "tensor", 1)
    near_far = swap(pieces[3], "tensor", 1)
    far = (pieces[2].astype(F32) + near_far.astype(F32)).astype(LOW)
    from_far = swap(far, "tensor", 2)
    return pieces[0].astype(F32) + near_own.astype(F32) + from_far.astype(F32)


def trade_pieces(pieces):
    return [pieces[0]] + [swap(pieces[r], "tensor", r) for r in range(1, 4)]


def sum_over_groups(values, turn):
    size = lax.axis_size("dp")
    place = lax.axis_index("dp")
    bits = [1 << b for b in range(size.bit_length() - 1)]
    bits = bits[turn:] + bits[:turn]
    values = values.astype(LOW)
    for bit in bits:
        half = values.shape[0] // 2
        side = (place // bit) % 2
        keep = lax.dynamic_slice_in_dim(values, side * half, half, 0)
        send = lax.dynamic_slice_in_dim(values, (1 - side) * half, half, 0)
        received = swap(send, "dp", bit)
        values = (keep.astype(F32) + received.astype(F32)).astype(LOW)
    for bit in reversed(bits):
        side = (place // bit) % 2
        received = swap(values, "dp", bit)
        values = jnp.where(
            side == 1,
            jnp.concatenate([received, values], 0),
            jnp.concatenate([values, received], 0),
        )
    return values.astype(F32)


def sum_everywhere(values):
    for axis in ("tensor", "dp"):
        size = lax.axis_size(axis)
        for b in range(size.bit_length() - 1):
            values = values + swap(values, axis, 1 << b)
    return values


def place_of(index, turn, per):
    return ((index // per) ^ turn) * per + index % per


def with_marks(values, marks):
    return jnp.concatenate([values[:, :128], values[:, 128:] + marks], axis=1)


def head_mask(shape, head, heads, keep_marks):
    lane = lax.broadcasted_iota(jnp.int32, shape, len(shape) - 1)
    own = lane // HEAD_DIM == head
    if keep_marks:
        own = own | (lane >= heads * HEAD_DIM)
    return own


def attend_kernel(
    plan, q_ref, k_ref, v_ref, qmark_ref, kmark_ref, *rest, heads, causal, blocks, per
):
    if causal:
        qframe_ref, kframe_ref, out_ref, stat_ref, top_s, acc_s = rest
    else:
        out_ref, stat_ref, top_s, acc_s = rest
    index = pl.program_id(1)
    turn = plan[0]
    marked = with_marks(q_ref[...] * LOW(HEAD_DIM**-0.5), qmark_ref[...])
    queries = [
        jnp.where(head_mask((BLOCK, WIDE), h, heads, True), marked, LOW(0)) for h in range(heads)
    ]
    lane = lax.broadcasted_iota(jnp.int32, (BLOCK, WIDE), 1)
    top_s[...] = jnp.full_like(top_s, -3.0e38)
    acc_s[...] = jnp.zeros_like(acc_s)

    def step(j, diagonal):
        row = pl.multiple_of(place_of(j, turn, per) * BLOCK, BLOCK)
        keys = with_marks(
            k_ref[pl.ds(row, BLOCK), :],
            kmark_ref[pl.ds(pl.multiple_of(j * BLOCK, BLOCK), BLOCK), :],
        )
        values = jnp.where(lane == heads * HEAD_DIM, LOW(1), v_ref[pl.ds(row, BLOCK), :])
        for h in range(heads):
            scores = dot(queries[h], keys, 1, 1)
            if diagonal:
                scores = jnp.where(kframe_ref[...] <= qframe_ref[...], scores, FAR)
            before = top_s[h]
            top = jnp.maximum(before, jnp.max(scores, axis=1, keepdims=True))
            weights = jnp.exp(scores - top[:, :1]).astype(LOW)
            shrink = jnp.exp(before - top)
            top_s[h] = top
            acc_s[h] = acc_s[h] * shrink[:, :1] + dot(weights, values, 1, 0)

    low = plan[1 + index]
    high = index if causal else plan[1 + blocks + index]

    def body(j, carry):
        step(j, False)
        return carry

    lax.fori_loop(low, high, body, 0)
    if causal:
        step(index, True)
    out = jnp.zeros((BLOCK, WIDE), F32)
    stats = jnp.zeros((BLOCK, 128), F32)
    for h in range(heads):
        total = acc_s[h][:, heads * HEAD_DIM : heads * HEAD_DIM + 1]
        out = jnp.where(head_mask((BLOCK, WIDE), h, heads, False), acc_s[h] / total, out)
        stats = jnp.where(
            lax.broadcasted_iota(jnp.int32, (BLOCK, 128), 1) == h,
            top_s[h] + jnp.log(total),
            stats,
        )
    out_ref[...] = out[:, : out_ref.shape[1]].astype(LOW)
    stat_ref[...] = stats.T[:8]


def attend(plan, qkv, lanes, marks, frames, out_cols, heads, repeat, per):
    q, k, v = qkv
    rows, keys = q.shape[0], k.shape[0]
    blocks = rows // BLOCK
    causal = frames is not None
    qmarks, kmarks = marks

    def turned(i, plan):
        return place_of(i, plan[0], per)

    in_specs = [
        pl.BlockSpec((BLOCK, WIDE), lambda r, i, plan: (turned(i, plan), lanes[0] + r)),
        pl.BlockSpec((keys, WIDE), lambda r, i, plan: (0, lanes[1] + r)),
        pl.BlockSpec((keys, WIDE), lambda r, i, plan: (0, lanes[2] + r)),
        pl.BlockSpec((BLOCK, 128), lambda r, i, plan: (i, 0)),
        pl.BlockSpec((keys, 128), lambda r, i, plan: (0, 0)),
    ]
    operands = [q, k, v, qmarks, kmarks]
    if causal:
        in_specs += [
            pl.BlockSpec((BLOCK, 1), lambda r, i, plan: (i, 0)),
            pl.BlockSpec((1, BLOCK), lambda r, i, plan: (0, i)),
        ]
        operands += [frames[:, None], frames[None, :]]
    area = rows * keys * heads * repeat // (3 if causal else 1)
    return pl.pallas_call(
        functools.partial(attend_kernel, heads=heads, causal=causal, blocks=blocks, per=per),
        grid_spec=pltpu.PrefetchScalarGridSpec(
            num_scalar_prefetch=1,
            grid=(repeat, blocks),
            in_specs=in_specs,
            out_specs=[
                pl.BlockSpec((BLOCK, out_cols), lambda r, i, plan: (turned(i, plan), r)),
                pl.BlockSpec((8, BLOCK), lambda r, i, plan: (r, i)),
            ],
            scratch_shapes=[
                pltpu.VMEM((heads, BLOCK, 128), F32),
                pltpu.VMEM((heads, BLOCK, WIDE), F32),
            ],
        ),
        out_shape=[
            jax.ShapeDtypeStruct((rows, out_cols * repeat), LOW),
            jax.ShapeDtypeStruct((8 * repeat, rows), F32),
        ],
        cost_estimate=pl.CostEstimate(
            flops=area * HEAD_DIM * 16, bytes_accessed=rows * 3000, transcendentals=area
        ),
        name="attend_self" if causal else "attend_cross",
    )(plan, *operands)


def attend_back_kernel(
    plan,
    q_ref,
    k_ref,
    v_ref,
    grad_ref,
    out_ref,
    stat_ref,
    qmark_ref,
    kmark_ref,
    *rest,
    heads,
    causal,
    blocks,
    key_blocks,
    per,
):
    if causal:
        qframe_ref, kframe_ref, *rest = rest
    dq_ref, dk_ref, dv_ref, q_s, g_s, inner_s, dq_s, dk_s, dv_s = rest
    j = pl.program_id(1)
    turn = plan[0]
    cols = heads * HEAD_DIM

    @pl.when(j == 0)
    def _():
        dq_s[...] = jnp.zeros_like(dq_s)

        def prepare(i, carry):
            spot = pl.ds(pl.multiple_of(i * BLOCK, BLOCK), BLOCK)
            row = pl.ds(pl.multiple_of(place_of(i, turn, per) * BLOCK, BLOCK), BLOCK)
            marked = with_marks(q_ref[row, :] * LOW(HEAD_DIM**-0.5), qmark_ref[spot, :])
            grads = grad_ref[row, :]
            product = grads[:, :cols].astype(F32) * out_ref[row, :][:, :cols].astype(F32)
            upper = product.astype(LOW)
            lower = (product - upper.astype(F32)).astype(LOW)
            lane = lax.broadcasted_iota(jnp.int32, (8, cols), 1)
            pick = (
                lane // HEAD_DIM == lax.broadcasted_iota(jnp.int32, (8, cols), 0)
            ).astype(LOW)
            inner_s[:, spot] = dot(pick, upper, 1, 1) + dot(pick, lower, 1, 1)
            for h in range(heads):
                mask = head_mask((BLOCK, WIDE), h, heads, True)
                q_s[h, spot, :] = jnp.where(mask, marked, LOW(0))
                g_s[h, spot, :] = jnp.where(
                    head_mask((BLOCK, WIDE), h, heads, False), grads, LOW(0)
                )
            return carry

        lax.fori_loop(0, blocks, prepare, 0)

    keys = k_ref[...]
    keys_turned = keys.astype(F32).T.astype(LOW)
    keys = with_marks(keys, kmark_ref[...])
    values = v_ref[...]
    dk_s[...] = jnp.zeros_like(dk_s)
    dv_s[...] = jnp.zeros_like(dv_s)

    def step(i, diagonal):
        spot = pl.ds(pl.multiple_of(i * BLOCK, BLOCK), BLOCK)
        for h in range(heads):
            queries = q_s[h, spot, :]
            grads = g_s[h, spot, :]
            scores = dot(keys, queries, 1, 1)
            if diagonal:
                scores = jnp.where(kframe_ref[...] <= qframe_ref[...], scores, FAR)
            weights = jnp.exp(scores - stat_ref[h : h + 1, spot])
            weight_grads = dot(values, grads, 1, 1)
            score_grads = (weights * (weight_grads - inner_s[h : h + 1, spot])).astype(LOW)
            dv_s[...] += dot(weights.astype(LOW), grads, 1, 0)
            dk_s[...] += dot(score_grads, queries, 1, 0)
            part = slice(h * HEAD_DIM, (h + 1) * HEAD_DIM)
            dq_s[part, spot] += dot(keys_turned[part], score_grads, 1, 0)

    low = j + 1 if causal else plan[1 + 2 * blocks + j]
    high = plan[1 + 2 * blocks + key_blocks + j]
    if causal:
        step(j, True)

    def body(i, carry):
        step(i, False)
        return carry

    lax.fori_loop(low, high, body, 0)
    dk_ref[...] = dk_s[...].astype(LOW)
    dv_ref[...] = dv_s[...].astype(LOW)

    @pl.when(j == key_blocks - 1)
    def _():
        def finish(i, carry):
            spot = pl.ds(pl.multiple_of(i * BLOCK, BLOCK), BLOCK)
            row = pl.ds(pl.multiple_of(place_of(i, turn, per) * BLOCK, BLOCK), BLOCK)
            dq_ref[row, :] = (dq_s[:, spot].T * HEAD_DIM**-0.5).astype(LOW)
            return carry

        lax.fori_loop(0, blocks, finish, 0)


def attend_back(plan, qkv, lanes, grads, out, out_cols, stats, marks, frames, heads, repeat, per):
    q, k, v = qkv
    rows, keys = q.shape[0], k.shape[0]
    blocks, key_blocks = rows // BLOCK, keys // BLOCK
    causal = frames is not None
    qmarks, kmarks = marks

    def turned(i, plan):
        return place_of(i, plan[0], per)

    in_specs = [
        pl.BlockSpec((rows, WIDE), lambda r, j, plan: (0, lanes[0] + r)),
        pl.BlockSpec((BLOCK, WIDE), lambda r, j, plan: (turned(j, plan), lanes[1] + r)),
        pl.BlockSpec((BLOCK, WIDE), lambda r, j, plan: (turned(j, plan), lanes[2] + r)),
        pl.BlockSpec((rows, WIDE), lambda r, j, plan: (0, r)),
        pl.BlockSpec((rows, out_cols), lambda r, j, plan: (0, r)),
        pl.BlockSpec((8, rows), lambda r, j, plan: (r, 0)),
        pl.BlockSpec((rows, 128), lambda r, j, plan: (0, 0)),
        pl.BlockSpec((BLOCK, 128), lambda r, j, plan: (j, 0)),
    ]
    operands = [q, k, v, grads, out, stats, qmarks, kmarks]
    if causal:
        in_specs += [
            pl.BlockSpec((1, BLOCK), lambda r, j, plan: (0, j)),
            pl.BlockSpec((BLOCK, 1), lambda r, j, plan: (j, 0)),
        ]
        operands += [frames[None, :], frames[:, None]]
    area = rows * keys * heads * repeat // (3 if causal else 1)
    return pl.pallas_call(
        functools.partial(
            attend_back_kernel,
            heads=heads,
            causal=causal,
            blocks=blocks,
            key_blocks=key_blocks,
            per=per,
        ),
        grid_spec=pltpu.PrefetchScalarGridSpec(
            num_scalar_prefetch=1,
            grid=(repeat, key_blocks),
            in_specs=in_specs,
            out_specs=[
                pl.BlockSpec((rows, WIDE), lambda r, j, plan: (0, r)),
                pl.BlockSpec((BLOCK, WIDE), lambda r, j, plan: (turned(j, plan), r)),
                pl.BlockSpec((BLOCK, WIDE), lambda r, j, plan: (turned(j, plan), r)),
            ],
            scratch_shapes=[
                pltpu.VMEM((heads, rows, WIDE), LOW),
                pltpu.VMEM((heads, rows, WIDE), LOW),
                pltpu.VMEM((8, rows), F32),
                pltpu.VMEM((WIDE, rows), F32),
                pltpu.VMEM((BLOCK, WIDE), F32),
                pltpu.VMEM((BLOCK, WIDE), F32),
            ],
        ),
        out_shape=[
            jax.ShapeDtypeStruct((rows, WIDE * repeat), LOW),
            jax.ShapeDtypeStruct((keys, WIDE * repeat), LOW),
            jax.ShapeDtypeStruct((keys, WIDE * repeat), LOW),
        ],
        cost_estimate=pl.CostEstimate(
            flops=area * HEAD_DIM * 40, bytes_accessed=rows * 6000, transcendentals=area
        ),
        name="attend_self_back" if causal else "attend_cross_back",
    )(plan, *operands)


def norm_forward(values, gain, bias):
    average = jnp.mean(values, axis=-1, keepdims=True)
    centred = values - average
    scale = lax.rsqrt(jnp.mean(centred * centred, axis=-1, keepdims=True) + EPSILON)
    return (centred * scale * gain + bias).astype(LOW), (average, scale)


def norm_backward(values, kept, gain, grad):
    average, scale = kept
    unit = (values - average) * scale
    inner = grad * gain
    into = scale * (
        inner
        - jnp.mean(inner, axis=-1, keepdims=True)
        - unit * jnp.mean(inner * unit, axis=-1, keepdims=True)
    )
    return into, jnp.sum(grad * unit, axis=0), jnp.sum(grad, axis=0)


def pad_cols(piece):
    return jnp.pad(piece, ((0, 0), (0, WIDE - piece.shape[1])))


def pad_rows(piece):
    return jnp.pad(piece, ((0, WIDE - piece.shape[0]), (0, 0)))


def gelu_pair(inputs):
    root = 0.7978845608028654
    square = inputs * inputs
    bend = jnp.tanh(root * (inputs + 0.044715 * inputs * square))
    value = 0.5 * inputs * (1.0 + bend)
    slope = 0.5 * (1.0 + bend) + 0.5 * inputs * (1.0 - bend * bend) * root * (
        1.0 + 3.0 * 0.044715 * square
    )
    return value.astype(LOW), slope.astype(LOW)


def shards(
    tokens,
    context,
    segment_ids,
    frame_ids,
    context_lengths,
    cross_gain,
    cross_bias,
    cross_query,
    cross_key,
    cross_value,
    cross_out,
    attn_gain,
    attn_bias,
    attn_query,
    attn_key,
    attn_value,
    attn_out,
    mlp_gain,
    mlp_bias,
    mlp_up,
    mlp_down,
    out_grad,
):
    turn = lax.axis_index("tensor")
    rows = tokens.shape[0]
    group_rows = segment_ids.shape[0]
    pieces = group_rows // rows
    cols = cross_query.shape[1]
    heads = cols // HEAD_DIM
    own_context = context.shape[0]
    context_rows = own_context * pieces

    clips = jnp.arange(context_lengths.shape[0], dtype=jnp.int32)
    clip_ends = jnp.cumsum(context_lengths).astype(jnp.int32)
    clip_starts = clip_ends - context_lengths
    context_ids = jnp.arange(context_rows, dtype=jnp.int32)
    context_clip = jnp.sum((context_ids[:, None] >= clip_ends[None, :]).astype(jnp.int32), axis=1)
    own_segments = lax.dynamic_slice_in_dim(segment_ids, turn * rows, rows, 0)
    mark_lane = jnp.arange(128, dtype=jnp.int32)[None, :] - (cols - 128)

    def query_marks(ids):
        return (mark_lane == ids[:, None]).astype(LOW)

    def key_marks(ids):
        inside = (mark_lane >= 0) & (mark_lane < clips.shape[0])
        return jnp.where(inside & (mark_lane != ids[:, None]), FAR, 0.0).astype(LOW)

    def count(flags):
        return jnp.sum(flags.astype(jnp.int32), axis=1)

    seg_first, seg_last = segment_ids[::BLOCK], segment_ids[BLOCK - 1 :: BLOCK]
    self_low = count(segment_ids[None, :] < seg_first[:, None]) // BLOCK
    self_high = (count(segment_ids[None, :] <= seg_last[:, None]) - 1) // BLOCK + 1
    here = jnp.zeros((1,), jnp.int32) + turn
    still = jnp.zeros((1,), jnp.int32)
    self_plan = jnp.concatenate([here, self_low, self_low, self_low, self_high])
    self_marks = (query_marks(segment_ids), key_marks(segment_ids))
    own_first, own_last = own_segments[::BLOCK], own_segments[BLOCK - 1 :: BLOCK]

    def at_clip(table, ids):
        return jnp.sum(jnp.where(ids[:, None] == clips[None, :], table[None, :], 0), axis=1)

    cross_low = at_clip(clip_starts, own_first) // BLOCK
    cross_high = (at_clip(clip_ends, own_last) - 1) // BLOCK + 1
    key_first, key_last = context_clip[::BLOCK], context_clip[BLOCK - 1 :: BLOCK]
    back_low = count(own_segments[None, :] < key_first[:, None]) // BLOCK
    back_high = (count(own_segments[None, :] <= key_last[:, None]) + BLOCK - 1) // BLOCK
    cross_plan = jnp.concatenate([still, cross_low, cross_high, back_low, back_high])
    cross_marks = (query_marks(own_segments), key_marks(context_clip))

    context_pieces = gather_pieces(context)
    query_pieces = gather_pieces(cross_query)
    context_all = jnp.zeros((context_rows, context.shape[1]), LOW)
    for r in range(4):
        context_all = lax.dynamic_update_slice_in_dim(
            context_all, context_pieces[r], (turn ^ r) * own_context, 0
        )
    pair_weight = jnp.concatenate([cross_key, cross_value], axis=1)
    pair = dot(context_all, pair_weight, 1, 0).astype(LOW)
    pair_pieces = gather_pieces(pair)
    out_pieces = gather_pieces(cross_out)
    start = tokens.astype(F32)
    normed1, kept1 = norm_forward(start, cross_gain, cross_bias)
    query_weight = jnp.concatenate([pad_cols(p) for p in query_pieces], axis=1)
    query1 = dot(normed1, query_weight, 1, 0).astype(LOW)
    key1 = jnp.concatenate([pad_cols(p[:, :cols]) for p in pair_pieces], axis=1)
    value1 = jnp.concatenate([pad_cols(p[:, cols:]) for p in pair_pieces], axis=1)
    mixed1, stats1 = attend(
        cross_plan, (query1, key1, value1), (0, 0, 0), cross_marks, None, WIDE, heads, 4, 1
    )
    out_weight1 = jnp.concatenate([pad_rows(p) for p in out_pieces], axis=0)
    hidden1 = start + dot(mixed1, out_weight1, 1, 0)

    normed2, kept2 = norm_forward(hidden1, attn_gain, attn_bias)
    normed2_all = jnp.concatenate(gather_pieces(normed2), axis=0)
    self_weight = jnp.concatenate(
        [pad_cols(attn_query), pad_cols(attn_key), pad_cols(attn_value)], axis=1
    )
    triple = dot(normed2_all, self_weight, 1, 0).astype(LOW)
    per = rows // BLOCK
    mixed2, stats2 = attend(
        self_plan, (triple, triple, triple), (0, 1, 2), self_marks, frame_ids, cols, heads, 1, per
    )
    out2_pieces = gather_pieces(attn_out)
    out_weight2 = jnp.concatenate([pad_rows(p) for p in out2_pieces], axis=0)
    mixed2_own = jnp.concatenate(
        [
            pad_cols(p)
            for p in trade_pieces([mixed2[r * rows : (r + 1) * rows] for r in range(4)])
        ],
        axis=1,
    )
    hidden2 = hidden1 + dot(mixed2_own, out_weight2, 1, 0)

    up_pieces = gather_pieces(mlp_up)
    down_pieces = gather_pieces(mlp_down)
    normed3, kept3 = norm_forward(hidden2, mlp_gain, mlp_bias)
    final = hidden2
    normed3_grad = jnp.zeros((rows, tokens.shape[1]), F32)
    down_grads, up_grads = [], []
    for r in range(4):
        activated, slope = gelu_pair(dot(normed3, up_pieces[r], 1, 0))
        final = final + dot(activated, down_pieces[r], 1, 0)
        upper_grad = (dot(out_grad, down_pieces[r], 1, 1) * slope.astype(F32)).astype(LOW)
        down_grads.append(dot(activated, out_grad, 0, 0))
        up_grads.append(dot(normed3, upper_grad, 0, 0))
        normed3_grad = normed3_grad + dot(upper_grad, up_pieces[r], 1, 1)
    block_out = final.astype(LOW)
    mlp_down_grad = sum_over_groups(reduce_pieces(down_grads), 0)
    mlp_up_grad = sum_over_groups(reduce_pieces(up_grads), 1)
    into3, mlp_gain_part, mlp_bias_part = norm_backward(hidden2, kept3, mlp_gain, normed3_grad)
    grad2 = out_grad.astype(F32) + into3

    grad2_low = grad2.astype(LOW)
    mixed2_grad = dot(grad2_low, out_weight2, 1, 1).astype(LOW)
    out2_grads = dot(mixed2_own, grad2_low, 0, 0)
    traded = trade_pieces([mixed2_grad[:, r * WIDE : r * WIDE + cols] for r in range(4)])
    traded = jnp.concatenate([pad_cols(p) for p in traded], axis=0)
    query2_grad, key2_grad, value2_grad = attend_back(
        self_plan,
        (triple, triple, triple),
        (0, 1, 2),
        traded,
        mixed2,
        cols,
        stats2,
        self_marks,
        frame_ids,
        heads,
        1,
        per,
    )
    triple_grad = jnp.concatenate([query2_grad, key2_grad, value2_grad], axis=1)
    normed2_parts = [
        dot(triple_grad[r * rows : (r + 1) * rows], self_weight, 1, 1) for r in range(4)
    ]
    normed2_grad = reduce_pieces(normed2_parts)
    self_weight_grad = dot(normed2_all, triple_grad, 0, 0)
    attn_out_grad = sum_over_groups(
        reduce_pieces([out2_grads[r * WIDE : r * WIDE + cols] for r in range(4)]), 0
    )
    triple_weight_grad = sum_over_groups(
        jnp.concatenate(
            [self_weight_grad[:, s * WIDE : s * WIDE + cols] for s in range(3)], axis=1
        ),
        1,
    )
    into2, attn_gain_part, attn_bias_part = norm_backward(hidden1, kept2, attn_gain, normed2_grad)
    grad1 = grad2 + into2

    grad1_low = grad1.astype(LOW)
    mixed1_grad = dot(grad1_low, out_weight1, 1, 1).astype(LOW)
    out1_grads = dot(mixed1, grad1_low, 0, 0)
    query1_grad, key1_grad, value1_grad = attend_back(
        cross_plan,
        (query1, key1, value1),
        (0, 0, 0),
        mixed1_grad,
        mixed1,
        WIDE,
        stats1,
        cross_marks,
        None,
        heads,
        4,
        1,
    )
    pair_grad = reduce_pieces(
        [
            jnp.concatenate(
                [key1_grad[:, r * WIDE : r * WIDE + cols], value1_grad[:, r * WIDE : r * WIDE + cols]],
                axis=1,
            )
            for r in range(4)
        ]
    ).astype(LOW)
    query_weight_grads = dot(normed1, query1_grad, 0, 0)
    normed1_grad = dot(query1_grad, query_weight, 1, 1)
    cross_out_grad = sum_over_groups(
        reduce_pieces([out1_grads[r * WIDE : r * WIDE + cols] for r in range(4)]), 0
    )
    pair_weight_grad = sum_over_groups(dot(context_all, pair_grad, 0, 0), 1)
    cross_query_grad = sum_over_groups(
        reduce_pieces([query_weight_grads[:, r * WIDE : r * WIDE + cols] for r in range(4)]), 0
    )
    context_part = dot(pair_grad, pair_weight, 1, 1)
    context_grad = reduce_pieces(
        [
            lax.dynamic_slice_in_dim(context_part, (turn ^ r) * own_context, own_context, 0)
            for r in range(4)
        ]
    )
    into1, cross_gain_part, cross_bias_part = norm_backward(
        start, kept1, cross_gain, normed1_grad
    )
    tokens_grad = grad1 + into1

    small = sum_everywhere(
        jnp.stack(
            [
                cross_gain_part,
                cross_bias_part,
                attn_gain_part,
                attn_bias_part,
                mlp_gain_part,
                mlp_bias_part,
            ]
        )
    )
    return (
        block_out,
        tokens_grad,
        context_grad,
        small[0],
        small[1],
        cross_query_grad,
        pair_weight_grad[:, :cols],
        pair_weight_grad[:, cols:],
        cross_out_grad,
        small[2],
        small[3],
        triple_weight_grad[:, :cols],
        triple_weight_grad[:, cols : 2 * cols],
        triple_weight_grad[:, 2 * cols :],
        attn_out_grad,
        small[4],
        small[5],
        mlp_up_grad,
        mlp_down_grad,
    )


def solution(mesh):
    in_specs = (
        P(("dp", "tensor"), None),
        P(("dp", "tensor"), None),
        P("dp"),
        P("dp"),
        P("dp"),
        P(),
        P(),
        P(None, "tensor"),
        P(None, "tensor"),
        P(None, "tensor"),
        P("tensor", None),
        P(),
        P(),
        P(None, "tensor"),
        P(None, "tensor"),
        P(None, "tensor"),
        P("tensor", None),
        P(),
        P(),
        P(None, "tensor"),
        P("tensor", None),
        P(("dp", "tensor"), None),
    )
    out_specs = (
        P(("dp", "tensor"), None),
        P(("dp", "tensor"), None),
        P(("dp", "tensor"), None),
        P(),
        P(),
        P(None, "tensor"),
        P(None, "tensor"),
        P(None, "tensor"),
        P("tensor", None),
        P(),
        P(),
        P(None, "tensor"),
        P(None, "tensor"),
        P(None, "tensor"),
        P("tensor", None),
        P(),
        P(),
        P(None, "tensor"),
        P("tensor", None),
    )
    return jax.shard_map(shards, mesh=mesh, in_specs=in_specs, out_specs=out_specs, check_vma=False)
```
